128 devices in a mesh: dp: 64 (over z, y, x), tensor: 2 (over core).
Axes of the slice: x: 4, y: 4, z: 4, core: 2. Of those that a mesh axis runs over, the one named last changes fastest.
Arguments:
- queries: bfloat16 [2, 1024, 7, 4096], P(None, 'dp', None, 'tensor'), may hold values from -120 to 120
- new_kv: bfloat16 [2, 2, 1024, 7, 512], P(None, None, 'dp', None, 'tensor'), may hold values from -9 to 9
- kv_cache: bfloat16 [2, 1024, 512, 512], P(None, 'dp', None, 'tensor'), may hold values from -9 to 9
- context_len: int32 [1024], P('dp'), may hold values from 64 to 512, as said below
- accepted: int32 [2, 1024], replicated, may hold values from 0 to 6, as said below
- residual: bfloat16 [2, 1024, 7, 8192], P(None, 'dp', None, 'tensor'), may hold values from -25 to 25
- out_weight: bfloat16 [4096, 8192], P('tensor'), may hold values from -0.09375 to 0.09375
- draft_gain: float32 [8192], P('tensor'), may hold values from 0.1 to 1.9
- draft_weight: bfloat16 [8192, 1024], P('tensor'), may hold values from -0.0625 to 0.0625
Outputs:
- draft_kv: bfloat16 [2, 8192, 1024], P(None, 'dp', 'tensor')
The draws below stay inside these ranges and needn't reach their ends.
Inputs may be any that keep to these rules, and one draw needn't show every extreme that they name: `context_len`: some conversation has exactly 512. `accepted`: in each step some conversation accepts all 6.
All inputs are finite; a program needn't handle non-finite values.
Results may differ from the reference program's by a relative error of at most 0.0025.
The reference program's roundings to bfloat16 on the way (of `weights`, `attended`, `hidden`, `scaled` and `new_rows`) count: a program that leaves them out, or rounds other values in their place, can miss the bound.
Values may be sent and summed in bfloat16 or wider, within the bound.
A program may use at most 192 MiB of HBM per device.

```python
import jax
import jax.numpy as jnp
from jax import lax

D = 8192
HEADS = 32
KVH = 4
DKVH = 4
HD = 128
DRAFT = 6
STEPS = 2
CONV_DEV = 16
CTX = 512
VER = 7
CONV = 1024
PEER_ROWS = 2
N_DP = 64


def cache_normal(key):
    drawn = jax.random.normal(jax.random.fold_in(key, 11), (2, CONV, CTX, KVH * HD), jnp.float32)
    return jnp.clip(drawn, -6.0, 6.0) * 1.5


def draw_kv_cache(key, part):
    cache = cache_normal(key)
    return cache.astype(jnp.bfloat16)


def draw_queries(key, part):
    drawn = 1.5 * jnp.clip(jax.random.normal(jax.random.fold_in(key, 13), (STEPS, CONV, VER, HEADS * HD), jnp.float32), -6.0, 6.0)
    return drawn.astype(jnp.bfloat16)


def draw_residual(key, part):
    values = 0.5 * jnp.clip(jax.random.normal(jax.random.fold_in(key, 24), (STEPS, CONV, VER, D), jnp.float32), -6.0, 6.0)
    return values.astype(jnp.bfloat16)


def draw_context_len(key, part):
    lengths = jax.random.randint(jax.random.fold_in(key, 31), (CONV,), CTX // 8, CTX + 1, jnp.int32)
    longest = jax.random.randint(jax.random.fold_in(key, 32), (), 0, CONV, jnp.int32)
    return lengths.at[longest].set(CTX)


def draw_accepted(key, part):
    first = jax.random.randint(jax.random.fold_in(key, 41), (STEPS, CONV), 0, DRAFT + 1, jnp.int32)
    second = jax.random.randint(jax.random.fold_in(key, 42), (STEPS, CONV), 0, DRAFT + 1, jnp.int32)
    counts = DRAFT - jnp.minimum(first, second)
    fullest = jax.random.randint(jax.random.fold_in(key, 43), (STEPS,), 0, CONV, jnp.int32)
    return counts.at[jnp.arange(STEPS), fullest].set(DRAFT)


def shard_levels(rng, shape, split, least, high):
    gain = 1.0
    for dim, parts in split:
        draws = jax.random.uniform(jax.random.fold_in(jax.random.fold_in(rng, 6), dim), (parts,), jnp.float32, least / len(split), high / len(split))
        gain = gain * jnp.repeat(jnp.exp(draws), shape[dim] // parts).reshape((-1,) + (1,) * (len(shape) - 1 - dim))
    return gain


def centred(own_key, shape, deviation, limit, pieces=(), held_as=jnp.bfloat16):
    loudness = shard_levels(own_key, shape, pieces, -0.22, 0.18) if pieces else 1.0
    values = jax.random.normal(own_key, shape, jnp.float32) * deviation * loudness
    return jnp.minimum(jnp.maximum(values, -limit), limit).astype(held_as)


def setup_inputs(seed: int = 0) -> dict:
    seeds = jax.random.split(jax.random.key(seed), 10)
    return {
        "queries": draw_queries(jax.random.fold_in(seeds[9], 71), 0),
        "new_kv": centred(seeds[1], (STEPS, 2, CONV, VER, KVH * HD), 1.5, 9.0, ((2, 64), (4, 2))),
        "kv_cache": draw_kv_cache(jax.random.fold_in(seeds[9], 71), 0),
        "context_len": draw_context_len(jax.random.fold_in(seeds[9], 71), 0),
        "accepted": draw_accepted(jax.random.fold_in(seeds[9], 71), 0),
        "residual": draw_residual(jax.random.fold_in(seeds[9], 71), 0),
        "out_weight": centred(seeds[6], (HEADS * HD, D), (HEADS * HD) ** -0.5, 0.09375, ((0, 2),)),
        "draft_gain": jnp.clip(1.0 + 0.18 * jax.random.normal(seeds[7], (D,), jnp.float32), 0.1, 1.9),
        "draft_weight": centred(seeds[8], (D, 2 * DKVH * HD), D ** -0.5, 0.0625, ((0, 2),)),
    }


def attend_one(query_rows, key_rows, value_rows, allowed):
    scores = jnp.einsum('ikgd,nkd->kgin', query_rows.astype(jnp.float32), key_rows.astype(jnp.float32)) * HD ** (-0.5)
    scores = jnp.where(allowed[None, None], scores, -jnp.inf)
    maximum = lax.optimization_barrier(jnp.max(scores, axis=-1, keepdims=True))
    expons = jnp.exp(scores - maximum)
    weights = (expons / lax.optimization_barrier(jnp.sum(expons, axis=-1, keepdims=True))).astype(jnp.bfloat16)
    attended = jnp.einsum('kgin,nkd->ikgd', weights.astype(jnp.float32), value_rows.astype(jnp.float32))
    return attended.astype(jnp.bfloat16).reshape(VER, HEADS * HD)

def reference(queries, new_kv, kv_cache, context_len, accepted, residual, out_weight, draft_gain, draft_weight):
    group_size = HEADS // KVH
    positions = jnp.arange(CTX, dtype=jnp.int32)
    block_index = jnp.arange(VER, dtype=jnp.int32)
    causal = block_index[None, :] <= block_index[:, None]
    row_total = CONV_DEV * VER
    draft_cols = 2 * DKVH * HD
    results = []
    for step_index in range(STEPS):
        if step_index > 0:
            earlier_kv = new_kv[step_index - 1]
            earlier_accepted = accepted[step_index - 1]
        else:
            earlier_kv = jnp.zeros_like(new_kv[0])
            earlier_accepted = jnp.full((CONV,), -1, jnp.int32)

        def per_conversation(inputs):
            query_rows, cache_keys, cache_values, old_keys, old_values, own_keys, own_values, length, earlier = inputs
            allowed = jnp.concatenate([jnp.broadcast_to(positions[None, :] < length, (VER, CTX)), jnp.broadcast_to(block_index[None, :] <= earlier, (VER, VER)), causal], axis=1)
            key_rows = jnp.concatenate([cache_keys, old_keys, own_keys], axis=0).reshape(-1, KVH, HD)
            value_rows = jnp.concatenate([cache_values, old_values, own_values], axis=0).reshape(-1, KVH, HD)
            return attend_one(query_rows.reshape(VER, KVH, group_size, HD), key_rows, value_rows, allowed)
        attended = lax.map(per_conversation, (queries[step_index], kv_cache[0], kv_cache[1], earlier_kv[0], earlier_kv[1], new_kv[step_index, 0], new_kv[step_index, 1], context_len, earlier_accepted))
        head_sum = jnp.dot(attended.reshape(CONV * VER, HEADS * HD), out_weight, preferred_element_type=jnp.float32)
        hidden = (residual[step_index].reshape(CONV * VER, D).astype(jnp.float32) + head_sum).astype(jnp.bfloat16)
        hidden_wide = hidden.astype(jnp.float32)
        squares = lax.optimization_barrier(jnp.mean(hidden_wide * hidden_wide, axis=-1, keepdims=True))
        scaled = (hidden_wide * draft_gain[None, :]).astype(jnp.bfloat16)
        projected = jnp.dot(scaled, draft_weight, preferred_element_type=jnp.float32)
        new_rows = (projected * lax.rsqrt(squares + 1e-05)).astype(jnp.bfloat16).reshape(CONV, VER, draft_cols)
        kept = block_index[None, :] <= accepted[step_index][:, None]
        new_rows = jnp.where(kept[:, :, None], new_rows, jnp.zeros_like(new_rows))
        by_source = new_rows.reshape(N_DP, row_total, draft_cols)
        by_source = jnp.pad(by_source, ((0, 0), (0, N_DP * PEER_ROWS - row_total), (0, 0)))
        ordered = by_source.reshape(N_DP, PEER_ROWS, N_DP, draft_cols).transpose(2, 0, 1, 3)
        results.append(ordered.reshape(N_DP * N_DP * PEER_ROWS, draft_cols))
    return jnp.stack(results, axis=0)
```

```python
import functools

import jax
import jax.numpy as jnp
from jax import lax
from jax.experimental import pallas as pl
from jax.experimental.pallas import tpu as pltpu
from jax.sharding import PartitionSpec as P

HD = 128
PADDED = 8
EXTRA = 128
SLOTS = 3
SENDS = 4
WIDE = 512
MESH = pl.DeviceIdType.MESH


def split_index(x, n):
    if n & (n - 1) == 0:
        shift = n.bit_length() - 1
        return x >> shift, x & (n - 1)
    if n == 7:
        top = (x * 9363) >> 16
        return top, x - top * n
    return x // n, x % n


def one_hot(have, want):
    return jnp.where(have == want, 1.0, 0.0).astype(jnp.bfloat16)


def fused_kernel(
    length_ref,
    accepted_ref,
    gain_ref,
    queries_hbm,
    new_kv_hbm,
    cache_hbm,
    residual_hbm,
    weight_hbm,
    draft_hbm,
    out_ref,
    row_v,
    pad_v,
    new_v,
    extra_v,
    k_v,
    v_v,
    hidden_v,
    weight_v,
    draft_v,
    spread_v,
    gather_v,
    perm_v,
    keep_v,
    send_v,
    recv_v,
    square_v,
    square_recv,
    ex_send,
    ex_recv,
    rows_v,
    packet_v,
    first_sem,
    pair_sem,
    weight_sem,
    draft_sem,
    send_sem,
    recv_sem,
    ex_send_sem,
    ex_recv_sem,
    row_send_sem,
    row_recv_sem,
    *,
    width,
    steps,
    conv,
    block,
):
    dp_count = out_ref.shape[0]
    ctx = cache_hbm.shape[2]
    head_cols = queries_hbm.shape[1]
    kv_local = cache_hbm.shape[3] // HD
    group = head_cols // HD // kv_local
    pairs = conv // 2
    chunks = recv_v.shape[0]
    step_rows = conv * block
    rows = steps * step_rows
    tall = steps * PADDED
    own_cols = draft_v.shape[2]
    quarters = own_cols // HD
    peer_rows = packet_v.shape[1] // (steps * quarters)
    me = lax.axis_index("dp")
    core = lax.axis_index("tensor")
    other = 1 - core

    def pair_copies(p):
        slot = lax.rem(p, SLOTS)
        span = pl.ds(p * 2, 2)
        return (
            pltpu.make_async_copy(
                cache_hbm.at[0, span], k_v.at[slot, :, pl.ds(0, ctx)], pair_sem.at[0, slot]
            ),
            pltpu.make_async_copy(
                cache_hbm.at[1, span], v_v.at[slot, :, pl.ds(0, ctx)], pair_sem.at[1, slot]
            ),
        )

    def weight_copy(c):
        side = jnp.where(c < chunks, other, core)
        at = pl.multiple_of(side * (chunks * WIDE) + lax.rem(c, chunks) * WIDE, WIDE)
        return pltpu.make_async_copy(
            weight_hbm.at[:, pl.ds(at, WIDE)], weight_v.at[c], weight_sem.at[c]
        )

    def draft_copy(half):
        side = other if half == 0 else core
        at = pl.multiple_of(side * own_cols, own_cols)
        return pltpu.make_async_copy(
            draft_hbm.at[:, pl.ds(at, own_cols)], draft_v.at[half], draft_sem.at[half]
        )

    query_copy = pltpu.make_async_copy(queries_hbm, row_v, first_sem.at[0])
    new_copy = pltpu.make_async_copy(new_kv_hbm, new_v, first_sem.at[1])
    residual_copy = pltpu.make_async_copy(residual_hbm, hidden_v, first_sem.at[2])
    query_copy.start()
    new_copy.start()
    for p in range(min(SLOTS - 1, pairs)):
        for copy in pair_copies(p):
            copy.start()

    barrier = pltpu.get_barrier_semaphore()
    pl.semaphore_signal(barrier, inc=1, device_id=(me, other), device_id_type=MESH)

    def greet(k, carry):
        pl.semaphore_signal(
            barrier, inc=1, device_id=(lax.rem(me + k, dp_count), core), device_id_type=MESH
        )
        return carry

    lax.fori_loop(1, dp_count, greet, 0)

    k_v[:, :, ctx + tall :, :] = jnp.zeros((SLOTS, 2, EXTRA - tall, kv_local * HD), jnp.bfloat16)
    v_v[:, :, ctx + tall :, :] = jnp.zeros((SLOTS, 2, EXTRA - tall, kv_local * HD), jnp.bfloat16)

    line = lax.broadcasted_iota(jnp.int32, (conv * tall, 1), 0)
    rest, place = split_index(line, PADDED)
    which, step = split_index(rest, steps)
    want = jnp.where(place < block, step * step_rows + place * conv + which, -1)
    spread_v[...] = one_hot(lax.broadcasted_iota(jnp.int32, spread_v.shape, 1), want)
    line = lax.broadcasted_iota(jnp.int32, (1, conv * tall), 1)
    rest, place = split_index(line, PADDED)
    which, step = split_index(rest, steps)
    want = jnp.where(place < block, step * step_rows + place * conv + which, -1)
    gather_v[...] = one_hot(lax.broadcasted_iota(jnp.int32, gather_v.shape, 0), want)

    perm_rows = perm_v.shape[0] // 8

    def make_perm(i, carry):
        line = lax.broadcasted_iota(jnp.int32, (perm_rows, 1), 0) + i * perm_rows
        rest, slot = split_index(line, peer_rows)
        rest, quarter = split_index(rest, quarters)
        peer, step = split_index(rest, steps)
        number = slot * dp_count + peer
        which, place = split_index(number, block)
        source = quarter * rows + step * step_rows + place * conv + which
        want = jnp.where(number < step_rows, source, -1)
        have = lax.broadcasted_iota(jnp.int32, (perm_rows, perm_v.shape[1]), 1)
        perm_v[pl.ds(i * perm_rows, perm_rows), :] = one_hot(have, want)
        return carry

    lax.fori_loop(0, 8, make_perm, 0)

    new_copy.wait()
    for part in range(2):
        extra_v[part] = jnp.dot(
            spread_v[...],
            jnp.concatenate([new_v[s, part] for s in range(steps)], axis=0),
            preferred_element_type=jnp.float32,
        ).astype(jnp.bfloat16)
    query_copy.wait()
    for c in range(head_cols // WIDE):
        lanes = slice(c * WIDE, (c + 1) * WIDE)
        pad_v[:, lanes] = jnp.dot(
            spread_v[...], row_v[:, lanes], preferred_element_type=jnp.float32
        ).astype(jnp.bfloat16)
    residual_copy.start()

    q_rows = group * tall
    scale = HD ** (-0.5) * 1.4426950408889634
    extra_row = lax.broadcasted_iota(jnp.int32, (q_rows, EXTRA), 0)
    extra_col = lax.broadcasted_iota(jnp.int32, (q_rows, EXTRA), 1)
    extra_line = extra_row & (PADDED - 1)
    second = (extra_row & PADDED) != 0
    first_keys = extra_col < PADDED
    own_limit = jnp.where(second == first_keys, -1, extra_line)
    own_limit = jnp.where(extra_col < tall, own_limit, -1)
    from_first = jnp.logical_and(second, first_keys)
    key_line = extra_col & (PADDED - 1)
    cache_col = lax.broadcasted_iota(jnp.int32, (1, ctx), 1)
    tall_line = lax.broadcasted_iota(jnp.int32, (tall, HD), 0)
    weights_each = (2 * chunks) // pairs

    def pair_body(p, carry):
        slot = lax.rem(p, SLOTS)

        @pl.when(p + SLOTS - 1 < pairs)
        def _():
            for copy in pair_copies(p + SLOTS - 1):
                copy.start()

        for w in range(weights_each):
            weight_copy(p * weights_each + w).start()
        for copy in pair_copies(p):
            copy.wait()

        for c in range(2):
            b = p * 2 + c
            at = pl.ds(pl.multiple_of(b * tall, tall), tall)
            k_v[slot, c, ctx : ctx + tall, :] = extra_v[0, at, :]
            v_v[slot, c, ctx : ctx + tall, :] = extra_v[1, at, :]
            took = [accepted_ref[s, me * conv + b] for s in range(steps)]
            keep_v[at, :] = jnp.where(
                (tall_line & (PADDED - 1)) <= jnp.where(tall_line < PADDED, took[0], took[1]),
                1.0,
                0.0,
            ).astype(jnp.bfloat16)
            q_wide = pad_v[at, :]
            for k in range(kv_local):
                lanes = slice(k * HD, (k + 1) * HD)
                q = jnp.concatenate(
                    [
                        q_wide[:, (k * group + h) * HD : (k * group + h + 1) * HD]
                        for h in range(group)
                    ],
                    axis=0,
                )
                scores = lax.dot_general(
                    q,
                    k_v[slot, c, :, lanes],
                    (((1,), (1,)), ((), ())),
                    preferred_element_type=jnp.float32,
                )
                cached = jnp.where(cache_col < length_ref[b], scores[:, :ctx], -jnp.inf)
                limit = jnp.where(from_first, took[0], own_limit)
                extra = jnp.where(key_line <= limit, scores[:, ctx:], -jnp.inf)
                top = jnp.maximum(
                    jnp.max(cached, axis=1, keepdims=True), jnp.max(extra, axis=1, keepdims=True)
                )
                top = top * scale
                cached = jnp.exp2(cached * scale - top)
                extra = jnp.exp2(extra * scale - top)
                total = jnp.sum(cached, axis=1, keepdims=True) + jnp.sum(
                    extra, axis=1, keepdims=True
                )
                inverse = 1.0 / total
                weights = jnp.concatenate([cached * inverse, extra * inverse], axis=1)
                result = jnp.dot(
                    weights.astype(jnp.bfloat16),
                    v_v[slot, c, :, lanes],
                    preferred_element_type=jnp.float32,
                ).astype(jnp.bfloat16)
                for h in range(group):
                    head = (k * group + h) * HD
                    pad_v[at, head : head + HD] = result[h * tall : (h + 1) * tall]
        return carry

    lax.fori_loop(0, pairs, pair_body, 0)
    for half in range(2):
        draft_copy(half).start()

    for c in range(head_cols // WIDE):
        lanes = slice(c * WIDE, (c + 1) * WIDE)
        row_v[:, lanes] = jnp.dot(
            gather_v[...], pad_v[:, lanes], preferred_element_type=jnp.float32
        ).astype(jnp.bfloat16)
    pl.semaphore_wait(barrier, dp_count)

    def partial_copy(c):
        slot = lax.rem(c, SENDS)
        return pltpu.make_async_remote_copy(
            src_ref=send_v.at[slot],
            dst_ref=recv_v.at[c],
            send_sem=send_sem.at[slot],
            recv_sem=recv_sem.at[c],
            device_id=(me, other),
            device_id_type=MESH,
        )

    def send_side(c, carry):
        weight_copy(c).wait()
        partial = jnp.dot(row_v[...], weight_v[c], preferred_element_type=jnp.float32)

        @pl.when(c >= SENDS)
        def _():
            partial_copy(c - SENDS).wait_send()

        send_v[lax.rem(c, SENDS)] = partial
        partial_copy(c).start()
        return carry

    lax.fori_loop(0, chunks, send_side, 0)
    square_v[...] = jnp.zeros(square_v.shape, jnp.float32)
    residual_copy.wait()

    def own_side(c, carry):
        weight_copy(c + chunks).wait()
        own = jnp.dot(row_v[...], weight_v[c + chunks], preferred_element_type=jnp.float32)
        at = pl.ds(pl.multiple_of(c * WIDE, WIDE), WIDE)
        own += hidden_v[:, at].astype(jnp.float32)
        partial_copy(c).wait_recv()
        hidden = (own + recv_v[c]).astype(jnp.bfloat16).astype(jnp.float32)
        squares = hidden * hidden
        part = square_v[...]
        for j in range(WIDE // HD):
            part += squares[:, j * HD : (j + 1) * HD]
        square_v[...] = part
        hidden_v[:, at] = (hidden * gain_ref[:, at]).astype(jnp.bfloat16)
        return carry

    lax.fori_loop(0, chunks, own_side, 0)

    def exchange(src, dst, n):
        return pltpu.make_async_remote_copy(
            src_ref=src,
            dst_ref=dst,
            send_sem=ex_send_sem.at[n],
            recv_sem=ex_recv_sem.at[n],
            device_id=(me, other),
            device_id_type=MESH,
        )

    square_copy = exchange(square_v, square_recv, 0)
    square_copy.start()
    draft_copy(0).wait()
    ex_send[...] = jnp.dot(hidden_v[...], draft_v[0], preferred_element_type=jnp.float32)
    draft_out = exchange(ex_send, ex_recv, 1)
    draft_out.start()
    draft_copy(1).wait()
    projected = jnp.dot(hidden_v[...], draft_v[1], preferred_element_type=jnp.float32)
    kept = jnp.dot(gather_v[...], keep_v[...], preferred_element_type=jnp.float32)
    square_copy.wait_recv()
    total = jnp.sum(square_v[...] + square_recv[...], axis=1, keepdims=True)
    factor = lax.rsqrt(total * (1.0 / width) + 1e-05)
    draft_out.wait_recv()
    projected = (projected + ex_recv[...]) * factor
    for j in range(quarters):
        piece = projected[:, j * HD : (j + 1) * HD]
        rows_v[j * rows : (j + 1) * rows, :] = jnp.where(kept > 0.5, piece, 0.0).astype(
            jnp.bfloat16
        )
    packets = jnp.dot(perm_v[...], rows_v[...], preferred_element_type=jnp.float32)
    packet_v[...] = packets.astype(jnp.bfloat16).reshape(packet_v.shape)

    def row_copy(src, dst, peer):
        return pltpu.make_async_remote_copy(
            src_ref=src,
            dst_ref=dst,
            send_sem=row_send_sem,
            recv_sem=row_recv_sem,
            device_id=(peer, core),
            device_id_type=MESH,
        )

    def scatter(k, carry):
        peer = lax.rem(me + k, dp_count)
        row_copy(packet_v.at[peer], out_ref.at[me], peer).start()
        return carry

    lax.fori_loop(1, dp_count, scatter, 0)
    out_ref[me] = packet_v[me]

    for c in range(max(0, chunks - SENDS), chunks):
        partial_copy(c).wait_send()
    square_copy.wait_send()
    draft_out.wait_send()
    most = pl.ds(0, dp_count - 1)
    everything = row_copy(packet_v.at[most], out_ref.at[most], other)
    everything.wait_send()
    everything.wait_recv()


def body(
    queries, new_kv, kv_cache, context_len, accepted, residual, out_weight, draft_gain, draft_weight
):
    dp_count = lax.axis_size("dp")
    steps, conv, block, head_cols = queries.shape
    ctx, kv_cols = kv_cache.shape[2:]
    d_cols = residual.shape[3]
    width = out_weight.shape[1]
    own_cols = draft_weight.shape[1] // 2
    quarters = own_cols // HD
    rows = steps * conv * block
    padded = steps * conv * PADDED
    peer_rows = -(-(conv * block) // dp_count)
    packet = steps * quarters * peer_rows
    chunks = d_cols // WIDE
    anywhere = pl.BlockSpec(memory_space=pl.ANY)
    smem = pl.BlockSpec(memory_space=pltpu.SMEM)
    vmem = pl.BlockSpec(memory_space=pltpu.VMEM)
    bf16, f32 = jnp.bfloat16, jnp.float32
    received = pl.pallas_call(
        functools.partial(fused_kernel, width=width, steps=steps, conv=conv, block=block),
        out_shape=jax.ShapeDtypeStruct((dp_count, packet, HD), bf16),
        in_specs=[smem, smem, vmem] + [anywhere] * 6,
        out_specs=vmem,
        scratch_shapes=[
            pltpu.VMEM((rows, head_cols), bf16),
            pltpu.VMEM((padded, head_cols), bf16),
            pltpu.VMEM((steps, 2, conv * block, kv_cols), bf16),
            pltpu.VMEM((2, padded, kv_cols), bf16),
            pltpu.VMEM((SLOTS, 2, ctx + EXTRA, kv_cols), bf16),
            pltpu.VMEM((SLOTS, 2, ctx + EXTRA, kv_cols), bf16),
            pltpu.VMEM((rows, d_cols), bf16),
            pltpu.VMEM((2 * chunks, head_cols, WIDE), bf16),
            pltpu.VMEM((2, d_cols, own_cols), bf16),
            pltpu.VMEM((padded, rows), bf16),
            pltpu.VMEM((rows, padded), bf16),
            pltpu.VMEM((dp_count * packet, quarters * rows), bf16),
            pltpu.VMEM((padded, HD), bf16),
            pltpu.VMEM((SENDS, rows, WIDE), f32),
            pltpu.VMEM((chunks, rows, WIDE), f32),
            pltpu.VMEM((rows, HD), f32),
            pltpu.VMEM((rows, HD), f32),
            pltpu.VMEM((rows, own_cols), f32),
            pltpu.VMEM((rows, own_cols), f32),
            pltpu.VMEM((quarters * rows, HD), bf16),
            pltpu.VMEM((dp_count, packet, HD), bf16),
            pltpu.SemaphoreType.DMA((3,)),
            pltpu.SemaphoreType.DMA((2, SLOTS)),
            pltpu.SemaphoreType.DMA((2 * chunks,)),
            pltpu.SemaphoreType.DMA((2,)),
            pltpu.SemaphoreType.DMA((SENDS,)),
            pltpu.SemaphoreType.DMA((chunks,)),
            pltpu.SemaphoreType.DMA((2,)),
            pltpu.SemaphoreType.DMA((2,)),
            pltpu.SemaphoreType.DMA,
            pltpu.SemaphoreType.DMA,
        ],
        compiler_params=pltpu.CompilerParams(
            collective_id=0, has_side_effects=True, vmem_limit_bytes=67043328
        ),
        name="verify_and_draft",
    )(
        context_len,
        accepted,
        draft_gain.reshape(1, d_cols),
        queries.transpose(0, 2, 1, 3).reshape(rows, head_cols),
        new_kv.transpose(0, 1, 3, 2, 4).reshape(steps, 2, conv * block, kv_cols),
        kv_cache,
        residual.transpose(0, 2, 1, 3).reshape(rows, d_cols),
        out_weight,
        draft_weight,
    )
    by_slot = received.reshape(dp_count, steps, quarters, peer_rows, HD)
    return by_slot.transpose(1, 0, 3, 2, 4).reshape(steps, dp_count * peer_rows, own_cols)


def solution(mesh):
    in_specs = (
        P(None, "dp", None, "tensor"),
        P(None, None, "dp", None, "tensor"),
        P(None, "dp", None, "tensor"),
        P("dp"),
        P(),
        P(None, "dp", None, "tensor"),
        P("tensor", None),
        P("tensor"),
        P("tensor", None),
    )
    out_specs = P(None, "dp", "tensor")
    return jax.shard_map(body, mesh=mesh, in_specs=in_specs, out_specs=out_specs, check_vma=False)
```

```python
import functools

import jax
import jax.numpy as jnp
from jax import lax
from jax.experimental import pallas as pl
from jax.experimental.pallas import tpu as pltpu
from jax.sharding import PartitionSpec as P

HD = 128
PADDED = 8
EXTRA = 128
SLOTS = 3
SENDS = 4
WIDE = 512
MESH = pl.DeviceIdType.MESH


def split_index(x, n):
    if n & (n - 1) == 0:
        shift = n.bit_length() - 1
        return x >> shift, x & (n - 1)
    if n == 7:
        top = (x * 9363) >> 16
        return top, x - top * n
    return x // n, x % n


def one_hot(have, want):
    return jnp.where(have == want, 1.0, 0.0).astype(jnp.bfloat16)


def fused_kernel(
    length_ref,
    accepted_ref,
    gain_ref,
    queries_hbm,
    new_kv_hbm,
    cache_hbm,
    residual_hbm,
    weight_hbm,
    draft_hbm,
    out_ref,
    row_v,
    pad_v,
    new_v,
    extra_v,
    k_v,
    v_v,
    hidden_v,
    weight_v,
    draft_v,
    spread_v,
    gather_v,
    perm_v,
    keep_v,
    send_v,
    recv_v,
    square_v,
    square_recv,
    ex_send,
    ex_recv,
    packet_v,
    first_sem,
    pair_sem,
    weight_sem,
    draft_sem,
    send_sem,
    recv_sem,
    ex_send_sem,
    ex_recv_sem,
    row_send_sem,
    row_recv_sem,
    *,
    width,
    steps,
    conv,
    block,
):
    dp_count = packet_v.shape[0]
    ctx = cache_hbm.shape[2]
    head_cols = queries_hbm.shape[1]
    kv_local = cache_hbm.shape[3] // HD
    group = head_cols // HD // kv_local
    pairs = conv // 2
    chunks = recv_v.shape[0]
    step_rows = conv * block
    rows = steps * step_rows
    tall = steps * PADDED
    own_cols = draft_v.shape[2]
    quarters = own_cols // HD
    peer_rows = packet_v.shape[3]
    fold = out_ref.shape[3]
    me = lax.axis_index("dp")
    core = lax.axis_index("tensor")
    other = 1 - core

    def pair_copies(p):
        slot = lax.rem(p, SLOTS)
        span = pl.ds(p * 2, 2)
        return (
            pltpu.make_async_copy(
                cache_hbm.at[0, span], k_v.at[slot, :, pl.ds(0, ctx)], pair_sem.at[0, slot]
            ),
            pltpu.make_async_copy(
                cache_hbm.at[1, span], v_v.at[slot, :, pl.ds(0, ctx)], pair_sem.at[1, slot]
            ),
        )

    def weight_copy(c):
        side = jnp.where(c < chunks, other, core)
        at = pl.multiple_of(side * (chunks * WIDE) + lax.rem(c, chunks) * WIDE, WIDE)
        return pltpu.make_async_copy(
            weight_hbm.at[:, pl.ds(at, WIDE)], weight_v.at[c], weight_sem.at[c]
        )

    def draft_copy(half):
        side = other if half == 0 else core
        at = pl.multiple_of(side * own_cols, own_cols)
        return pltpu.make_async_copy(
            draft_hbm.at[:, pl.ds(at, own_cols)], draft_v.at[half], draft_sem.at[half]
        )

    query_copy = pltpu.make_async_copy(queries_hbm, row_v, first_sem.at[0])
    new_copy = pltpu.make_async_copy(new_kv_hbm, new_v, first_sem.at[1])
    residual_copy = pltpu.make_async_copy(residual_hbm, hidden_v, first_sem.at[2])
    query_copy.start()
    new_copy.start()
    for p in range(min(SLOTS - 1, pairs)):
        for copy in pair_copies(p):
            copy.start()

    barrier = pltpu.get_barrier_semaphore()
    pl.semaphore_signal(barrier, inc=1, device_id=(me, other), device_id_type=MESH)

    def greet(k, carry):
        pl.semaphore_signal(
            barrier, inc=1, device_id=(lax.rem(me + k, dp_count), core), device_id_type=MESH
        )
        return carry

    lax.fori_loop(1, dp_count, greet, 0)

    k_v[:, :, ctx + tall :, :] = jnp.zeros((SLOTS, 2, EXTRA - tall, kv_local * HD), jnp.bfloat16)
    v_v[:, :, ctx + tall :, :] = jnp.zeros((SLOTS, 2, EXTRA - tall, kv_local * HD), jnp.bfloat16)

    line = lax.broadcasted_iota(jnp.int32, (conv * tall, 1), 0)
    rest, place = split_index(line, PADDED)
    which, step = split_index(rest, steps)
    want = jnp.where(place < block, step * step_rows + place * conv + which, -1)
    spread_v[...] = one_hot(lax.broadcasted_iota(jnp.int32, spread_v.shape, 1), want)
    line = lax.broadcasted_iota(jnp.int32, (1, conv * tall), 1)
    rest, place = split_index(line, PADDED)
    which, step = split_index(rest, steps)
    want = jnp.where(place < block, step * step_rows + place * conv + which, -1)
    gather_v[...] = one_hot(lax.broadcasted_iota(jnp.int32, gather_v.shape, 0), want)

    line = lax.broadcasted_iota(jnp.int32, (perm_v.shape[0], 1), 0)
    rest, slot = split_index(line, peer_rows)
    peer, step = split_index(rest, steps)
    number = slot * dp_count + peer
    which, place = split_index(number, block)
    want = jnp.where(number < step_rows, step * step_rows + place * conv + which, -1)
    perm_v[...] = one_hot(lax.broadcasted_iota(jnp.int32, perm_v.shape, 1), want)

    new_copy.wait()
    for part in range(2):
        extra_v[part] = jnp.dot(
            spread_v[...],
            jnp.concatenate([new_v[s, part] for s in range(steps)], axis=0),
            preferred_element_type=jnp.float32,
        ).astype(jnp.bfloat16)
    query_copy.wait()
    for c in range(head_cols // WIDE):
        lanes = slice(c * WIDE, (c + 1) * WIDE)
        pad_v[:, lanes] = jnp.dot(
            spread_v[...], row_v[:, lanes], preferred_element_type=jnp.float32
        ).astype(jnp.bfloat16)
    residual_copy.start()

    q_rows = group * tall
    scale = HD ** (-0.5) * 1.4426950408889634
    extra_row = lax.broadcasted_iota(jnp.int32, (q_rows, EXTRA), 0)
    extra_col = lax.broadcasted_iota(jnp.int32, (q_rows, EXTRA), 1)
    extra_line = extra_row & (PADDED - 1)
    second = (extra_row & PADDED) != 0
    first_keys = extra_col < PADDED
    own_limit = jnp.where(second == first_keys, -1, extra_line)
    own_limit = jnp.where(extra_col < tall, own_limit, -1)
    from_first = jnp.logical_and(second, first_keys)
    key_line = extra_col & (PADDED - 1)
    cache_col = lax.broadcasted_iota(jnp.int32, (1, ctx), 1)
    tall_line = lax.broadcasted_iota(jnp.int32, (tall, HD), 0)
    weights_each = (2 * chunks) // pairs

    def pair_body(p, carry):
        slot = lax.rem(p, SLOTS)

        @pl.when(p + SLOTS - 1 < pairs)
        def _():
            for copy in pair_copies(p + SLOTS - 1):
                copy.start()

        for w in range(weights_each):
            weight_copy(p * weights_each + w).start()
        for copy in pair_copies(p):
            copy.wait()

        for c in range(2):
            b = p * 2 + c
            at = pl.ds(pl.multiple_of(b * tall, tall), tall)
            k_v[slot, c, ctx : ctx + tall, :] = extra_v[0, at, :]
            v_v[slot, c, ctx : ctx + tall, :] = extra_v[1, at, :]
            took = [accepted_ref[s, me * conv + b] for s in range(steps)]
            keep_v[at, :] = jnp.where(
                (tall_line & (PADDED - 1)) <= jnp.where(tall_line < PADDED, took[0], took[1]),
                1.0,
                0.0,
            ).astype(jnp.bfloat16)
            q_wide = pad_v[at, :]
            for k in range(kv_local):
                lanes = slice(k * HD, (k + 1) * HD)
                q = jnp.concatenate(
                    [
                        q_wide[:, (k * group + h) * HD : (k * group + h + 1) * HD]
                        for h in range(group)
                    ],
                    axis=0,
                )
                scores = lax.dot_general(
                    q,
                    k_v[slot, c, :, lanes],
                    (((1,), (1,)), ((), ())),
                    preferred_element_type=jnp.float32,
                )
                cached = jnp.where(cache_col < length_ref[b], scores[:, :ctx], -jnp.inf)
                limit = jnp.where(from_first, took[0], own_limit)
                extra = jnp.where(key_line <= limit, scores[:, ctx:], -jnp.inf)
                top = jnp.maximum(
                    jnp.max(cached, axis=1, keepdims=True), jnp.max(extra, axis=1, keepdims=True)
                )
                top = top * scale
                cached = jnp.exp2(cached * scale - top)
                extra = jnp.exp2(extra * scale - top)
                total = jnp.sum(cached, axis=1, keepdims=True) + jnp.sum(
                    extra, axis=1, keepdims=True
                )
                inverse = 1.0 / total
                weights = jnp.concatenate([cached * inverse, extra * inverse], axis=1)
                result = jnp.dot(
                    weights.astype(jnp.bfloat16),
                    v_v[slot, c, :, lanes],
                    preferred_element_type=jnp.float32,
                ).astype(jnp.bfloat16)
                for h in range(group):
                    head = (k * group + h) * HD
                    pad_v[at, head : head + HD] = result[h * tall : (h + 1) * tall]
        return carry

    lax.fori_loop(0, pairs, pair_body, 0)
    for half in range(2):
        draft_copy(half).start()

    for c in range(head_cols // WIDE):
        lanes = slice(c * WIDE, (c + 1) * WIDE)
        row_v[:, lanes] = jnp.dot(
            gather_v[...], pad_v[:, lanes], preferred_element_type=jnp.float32
        ).astype(jnp.bfloat16)
    pl.semaphore_wait(barrier, dp_count)

    def partial_copy(c):
        slot = lax.rem(c, SENDS)
        return pltpu.make_async_remote_copy(
            src_ref=send_v.at[slot],
            dst_ref=recv_v.at[c],
            send_sem=send_sem.at[slot],
            recv_sem=recv_sem.at[c],
            device_id=(me, other),
            device_id_type=MESH,
        )

    def send_side(c, carry):
        weight_copy(c).wait()
        partial = jnp.dot(row_v[...], weight_v[c], preferred_element_type=jnp.float32)

        @pl.when(c >= SENDS)
        def _():
            partial_copy(c - SENDS).wait_send()

        send_v[lax.rem(c, SENDS)] = partial
        partial_copy(c).start()
        return carry

    lax.fori_loop(0, chunks, send_side, 0)
    square_v[...] = jnp.zeros(square_v.shape, jnp.float32)
    residual_copy.wait()

    def own_side(c, carry):
        weight_copy(c + chunks).wait()
        own = jnp.dot(row_v[...], weight_v[c + chunks], preferred_element_type=jnp.float32)
        at = pl.ds(pl.multiple_of(c * WIDE, WIDE), WIDE)
        own += hidden_v[:, at].astype(jnp.float32)
        partial_copy(c).wait_recv()
        hidden = (own + recv_v[c]).astype(jnp.bfloat16).astype(jnp.float32)
        squares = hidden * hidden
        part = square_v[...]
        for j in range(WIDE // HD):
            part += squares[:, j * HD : (j + 1) * HD]
        square_v[...] = part
        hidden_v[:, at] = (hidden * gain_ref[:, at]).astype(jnp.bfloat16)
        return carry

    lax.fori_loop(0, chunks, own_side, 0)

    def exchange(src, dst, n):
        return pltpu.make_async_remote_copy(
            src_ref=src,
            dst_ref=dst,
            send_sem=ex_send_sem.at[n],
            recv_sem=ex_recv_sem.at[n],
            device_id=(me, other),
            device_id_type=MESH,
        )

    square_copy = exchange(square_v, square_recv, 0)
    square_copy.start()
    draft_copy(0).wait()
    ex_send[...] = jnp.dot(hidden_v[...], draft_v[0], preferred_element_type=jnp.float32)
    draft_out = exchange(ex_send, ex_recv, 1)
    draft_out.start()
    draft_copy(1).wait()
    projected = jnp.dot(hidden_v[...], draft_v[1], preferred_element_type=jnp.float32)
    kept = jnp.dot(gather_v[...], keep_v[...], preferred_element_type=jnp.float32)
    square_copy.wait_recv()
    total = jnp.sum(square_v[...] + square_recv[...], axis=1, keepdims=True)
    factor = lax.rsqrt(total * (1.0 / width) + 1e-05)
    draft_out.wait_recv()
    projected = (projected + ex_recv[...]) * factor
    new_rows = jnp.where(kept[:, :1] > 0.5, projected, 0.0).astype(jnp.bfloat16)
    packets = jnp.dot(perm_v[...], new_rows, preferred_element_type=jnp.float32)
    packets = packets.astype(jnp.bfloat16)
    for j in range(quarters):
        piece = packets[:, j * HD : (j + 1) * HD]
        packet_v[:, :, j] = piece.reshape(dp_count, steps, peer_rows, HD)

    def row_copy(src, dst, peer):
        return pltpu.make_async_remote_copy(
            src_ref=src,
            dst_ref=dst,
            send_sem=row_send_sem,
            recv_sem=row_recv_sem,
            device_id=(peer, core),
            device_id_type=MESH,
        )

    side = round(dp_count ** (1 / 3))
    digits = [[lax.rem(me // side**a + d, side) * side**a for d in range(side)] for a in range(3)]
    hops = [min(d, side - d) for d in range(side)]
    offsets = [(a, b, c) for a in range(side) for b in range(side) for c in range(side)]
    offsets.sort(key=lambda o: -sum(hops[d] for d in o))
    top, low = me // fold, lax.rem(me, fold)
    for a, b, c in offsets[:-1]:
        peer = digits[2][a] + digits[1][b] + digits[0][c]
        row_copy(packet_v.at[peer], out_ref.at[:, top, :, low], peer).start()
    out_ref[:, top, :, low] = packet_v[me]

    for c in range(max(0, chunks - SENDS), chunks):
        partial_copy(c).wait_send()
    square_copy.wait_send()
    draft_out.wait_send()
    most = pl.ds(0, dp_count - 1)
    everything = row_copy(packet_v.at[most], packet_v.at[most], other)
    everything.wait_send()
    everything.wait_recv()


def body(
    queries, new_kv, kv_cache, context_len, accepted, residual, out_weight, draft_gain, draft_weight
):
    dp_count = lax.axis_size("dp")
    steps, conv, block, head_cols = queries.shape
    ctx, kv_cols = kv_cache.shape[2:]
    d_cols = residual.shape[3]
    width = out_weight.shape[1]
    own_cols = draft_weight.shape[1] // 2
    quarters = own_cols // HD
    rows = steps * conv * block
    padded = steps * conv * PADDED
    peer_rows = -(-(conv * block) // dp_count)
    fold = 8 // peer_rows
    chunks = d_cols // WIDE
    anywhere = pl.BlockSpec(memory_space=pl.ANY)
    smem = pl.BlockSpec(memory_space=pltpu.SMEM)
    vmem = pl.BlockSpec(memory_space=pltpu.VMEM)
    bf16, f32 = jnp.bfloat16, jnp.float32
    received = pl.pallas_call(
        functools.partial(fused_kernel, width=width, steps=steps, conv=conv, block=block),
        out_shape=jax.ShapeDtypeStruct(
            (steps, dp_count // fold, quarters, fold, peer_rows, HD), bf16
        ),
        in_specs=[smem, smem, vmem] + [anywhere] * 6,
        out_specs=vmem,
        scratch_shapes=[
            pltpu.VMEM((rows, head_cols), bf16),
            pltpu.VMEM((padded, head_cols), bf16),
            pltpu.VMEM((steps, 2, conv * block, kv_cols), bf16),
            pltpu.VMEM((2, padded, kv_cols), bf16),
            pltpu.VMEM((SLOTS, 2, ctx + EXTRA, kv_cols), bf16),
            pltpu.VMEM((SLOTS, 2, ctx + EXTRA, kv_cols), bf16),
            pltpu.VMEM((rows, d_cols), bf16),
            pltpu.VMEM((2 * chunks, head_cols, WIDE), bf16),
            pltpu.VMEM((2, d_cols, own_cols), bf16),
            pltpu.VMEM((padded, rows), bf16),
            pltpu.VMEM((rows, padded), bf16),
            pltpu.VMEM((dp_count * steps * peer_rows, rows), bf16),
            pltpu.VMEM((padded, HD), bf16),
            pltpu.VMEM((SENDS, rows, WIDE), f32),
            pltpu.VMEM((chunks, rows, WIDE), f32),
            pltpu.VMEM((rows, HD), f32),
            pltpu.VMEM((rows, HD), f32),
            pltpu.VMEM((rows, own_cols), f32),
            pltpu.VMEM((rows, own_cols), f32),
            pltpu.VMEM((dp_count, steps, quarters, peer_rows, HD), bf16),
            pltpu.SemaphoreType.DMA((3,)),
            pltpu.SemaphoreType.DMA((2, SLOTS)),
            pltpu.SemaphoreType.DMA((2 * chunks,)),
            pltpu.SemaphoreType.DMA((2,)),
            pltpu.SemaphoreType.DMA((SENDS,)),
            pltpu.SemaphoreType.DMA((chunks,)),
            pltpu.SemaphoreType.DMA((2,)),
            pltpu.SemaphoreType.DMA((2,)),
            pltpu.SemaphoreType.DMA,
            pltpu.SemaphoreType.DMA,
        ],
        compiler_params=pltpu.CompilerParams(
            collective_id=0, has_side_effects=True, vmem_limit_bytes=67043328
        ),
        name="verify_and_draft",
    )(
        context_len,
        accepted,
        draft_gain.reshape(1, d_cols),
        queries.transpose(0, 2, 1, 3).reshape(rows, head_cols),
        new_kv.transpose(0, 1, 3, 2, 4).reshape(steps, 2, conv * block, kv_cols),
        kv_cache,
        residual.transpose(0, 2, 1, 3).reshape(rows, d_cols),
        out_weight,
        draft_weight,
    )
    by_row = received.transpose(0, 1, 3, 4, 2, 5)
    return by_row.reshape(steps, dp_count * peer_rows, own_cols)


def solution(mesh):
    in_specs = (
        P(None, "dp", None, "tensor"),
        P(None, None, "dp", None, "tensor"),
        P(None, "dp", None, "tensor"),
        P("dp"),
        P(),
        P(None, "dp", None, "tensor"),
        P("tensor", None),
        P("tensor"),
        P("tensor", None),
    )
    out_specs = P(None, "dp", "tensor")
    return jax.shard_map(body, mesh=mesh, in_specs=in_specs, out_specs=out_specs, check_vma=False)
```

```python
import functools

import jax
import jax.numpy as jnp
from jax import lax
from jax.experimental import pallas as pl
from jax.experimental.pallas import tpu as pltpu
from jax.sharding import PartitionSpec as P

HD = 128
PADDED = 8
EXTRA = 128
SLOTS = 3
SENDS = 4
WIDE = 512
MESH = pl.DeviceIdType.MESH


def split_index(x, n):
    if n & (n - 1) == 0:
        shift = n.bit_length() - 1
        return x >> shift, x & (n - 1)
    if n == 7:
        top = (x * 9363) >> 16
        return top, x - top * n
    return x // n, x % n


def one_hot(have, want):
    return jnp.where(have == want, 1.0, 0.0).astype(jnp.bfloat16)


def fused_kernel(
    length_ref,
    accepted_ref,
    gain_ref,
    queries_hbm,
    new_kv_hbm,
    cache_hbm,
    residual_hbm,
    weight_hbm,
    draft_hbm,
    out_ref,
    row_v,
    pad_v,
    new_v,
    extra_v,
    k_v,
    v_v,
    hidden_v,
    weight_v,
    draft_v,
    spread_v,
    gather_v,
    perm_v,
    keep_v,
    send_v,
    recv_v,
    square_v,
    square_recv,
    ex_send,
    ex_recv,
    packet_v,
    first_sem,
    pair_sem,
    weight_sem,
    draft_sem,
    send_sem,
    recv_sem,
    ex_send_sem,
    ex_recv_sem,
    row_send_sem,
    row_recv_sem,
    *,
    width,
    steps,
    conv,
    block,
):
    dp_count = packet_v.shape[0]
    ctx = cache_hbm.shape[2]
    head_cols = queries_hbm.shape[1]
    kv_local = cache_hbm.shape[3] // HD
    group = head_cols // HD // kv_local
    pairs = conv // 2
    chunks = recv_v.shape[0]
    step_rows = conv * block
    rows = steps * step_rows
    tall = steps * PADDED
    own_cols = draft_v.shape[2]
    quarters = own_cols // HD
    peer_rows = packet_v.shape[3]
    fold = out_ref.shape[3]
    me = lax.axis_index("dp")
    core = lax.axis_index("tensor")
    other = 1 - core

    def pair_copies(p):
        slot = lax.rem(p, SLOTS)
        span = pl.ds(p * 2, 2)
        return (
            pltpu.make_async_copy(
                cache_hbm.at[0, span], k_v.at[slot, :, pl.ds(0, ctx)], pair_sem.at[0, slot]
            ),
            pltpu.make_async_copy(
                cache_hbm.at[1, span], v_v.at[slot, :, pl.ds(0, ctx)], pair_sem.at[1, slot]
            ),
        )

    def weight_copy(c):
        side = jnp.where(c < chunks, other, core)
        at = pl.multiple_of(side * (chunks * WIDE) + lax.rem(c, chunks) * WIDE, WIDE)
        return pltpu.make_async_copy(
            weight_hbm.at[:, pl.ds(at, WIDE)], weight_v.at[c], weight_sem.at[c]
        )

    def draft_copy(half):
        side = other if half == 0 else core
        at = pl.multiple_of(side * own_cols, own_cols)
        return pltpu.make_async_copy(
            draft_hbm.at[:, pl.ds(at, own_cols)], draft_v.at[half], draft_sem.at[half]
        )

    query_copy = pltpu.make_async_copy(queries_hbm, row_v, first_sem.at[0])
    new_copy = pltpu.make_async_copy(new_kv_hbm, new_v, first_sem.at[1])
    residual_copy = pltpu.make_async_copy(residual_hbm, hidden_v, first_sem.at[2])
    query_copy.start()
    new_copy.start()
    for p in range(min(SLOTS - 1, pairs)):
        for copy in pair_copies(p):
            copy.start()

    barrier = pltpu.get_barrier_semaphore()
    pl.semaphore_signal(barrier, inc=1, device_id=(me, other), device_id_type=MESH)

    def greet(k, carry):
        pl.semaphore_signal(
            barrier, inc=1, device_id=(lax.rem(me + k, dp_count), core), device_id_type=MESH
        )
        return carry

    lax.fori_loop(1, dp_count, greet, 0)

    k_v[:, :, ctx + tall :, :] = jnp.zeros((SLOTS, 2, EXTRA - tall, kv_local * HD), jnp.bfloat16)
    v_v[:, :, ctx + tall :, :] = jnp.zeros((SLOTS, 2, EXTRA - tall, kv_local * HD), jnp.bfloat16)

    line = lax.broadcasted_iota(jnp.int32, (conv * tall, 1), 0)
    rest, place = split_index(line, PADDED)
    which, step = split_index(rest, steps)
    want = jnp.where(place < block, step * step_rows + place * conv + which, -1)
    spread_v[...] = one_hot(lax.broadcasted_iota(jnp.int32, spread_v.shape, 1), want)
    line = lax.broadcasted_iota(jnp.int32, (1, conv * tall), 1)
    rest, place = split_index(line, PADDED)
    which, step = split_index(rest, steps)
    want = jnp.where(place < block, step * step_rows + place * conv + which, -1)
    gather_v[...] = one_hot(lax.broadcasted_iota(jnp.int32, gather_v.shape, 0), want)

    line = lax.broadcasted_iota(jnp.int32, (perm_v.shape[0], 1), 0)
    rest, slot = split_index(line, peer_rows)
    peer, step = split_index(rest, steps)
    number = slot * dp_count + peer
    which, place = split_index(number, block)
    want = jnp.where(number < step_rows, step * step_rows + place * conv + which, -1)
    perm_v[...] = one_hot(lax.broadcasted_iota(jnp.int32, perm_v.shape, 1), want)

    new_copy.wait()
    for part in range(2):
        extra_v[part] = jnp.dot(
            spread_v[...],
            jnp.concatenate([new_v[s, part] for s in range(steps)], axis=0),
            preferred_element_type=jnp.float32,
        ).astype(jnp.bfloat16)
    query_copy.wait()
    for c in range(head_cols // WIDE):
        lanes = slice(c * WIDE, (c + 1) * WIDE)
        pad_v[:, lanes] = jnp.dot(
            spread_v[...], row_v[:, lanes], preferred_element_type=jnp.float32
        ).astype(jnp.bfloat16)
    residual_copy.start()

    q_rows = group * tall
    scale = HD ** (-0.5) * 1.4426950408889634
    extra_row = lax.broadcasted_iota(jnp.int32, (q_rows, EXTRA), 0)
    extra_col = lax.broadcasted_iota(jnp.int32, (q_rows, EXTRA), 1)
    extra_line = extra_row & (PADDED - 1)
    second = (extra_row & PADDED) != 0
    first_keys = extra_col < PADDED
    own_limit = jnp.where(second == first_keys, -1, extra_line)
    own_limit = jnp.where(extra_col < tall, own_limit, -1)
    from_first = jnp.logical_and(second, first_keys)
    key_line = extra_col & (PADDED - 1)
    cache_col = lax.broadcasted_iota(jnp.int32, (1, ctx), 1)
    tall_line = lax.broadcasted_iota(jnp.int32, (tall, HD), 0)
    weights_each = (2 * chunks) // pairs

    def pair_body(p, carry):
        slot = lax.rem(p, SLOTS)

        @pl.when(p + SLOTS - 1 < pairs)
        def _():
            for copy in pair_copies(p + SLOTS - 1):
                copy.start()

        for w in range(weights_each):
            weight_copy(p * weights_each + w).start()
        for copy in pair_copies(p):
            copy.wait()

        units = []
        for c in range(2):
            b = p * 2 + c
            at = pl.ds(pl.multiple_of(b * tall, tall), tall)
            k_v[slot, c, ctx : ctx + tall, :] = extra_v[0, at, :]
            v_v[slot, c, ctx : ctx + tall, :] = extra_v[1, at, :]
            took = [accepted_ref[s, me * conv + b] for s in range(steps)]
            keep_v[at, :] = jnp.where(
                (tall_line & (PADDED - 1)) <= jnp.where(tall_line < PADDED, took[0], took[1]),
                1.0,
                0.0,
            ).astype(jnp.bfloat16)
            limit = jnp.where(from_first, took[0], own_limit)
            q_wide = pad_v[at, :]
            for k in range(kv_local):
                units.append((c, k, at, cache_col < length_ref[b], key_line <= limit, q_wide))

        def score(unit):
            c, k, _, _, _, q_wide = unit
            q = jnp.concatenate(
                [q_wide[:, (k * group + h) * HD : (k * group + h + 1) * HD] for h in range(group)],
                axis=0,
            )
            return lax.dot_general(
                q,
                k_v[slot, c, :, k * HD : (k + 1) * HD],
                (((1,), (1,)), ((), ())),
                preferred_element_type=jnp.float32,
            )

        def attend(unit, scores):
            c, k, _, valid, allowed, _ = unit
            cached = jnp.where(valid, scores[:, :ctx], -jnp.inf)
            extra = jnp.where(allowed, scores[:, ctx:], -jnp.inf)
            top = jnp.maximum(
                jnp.max(cached, axis=1, keepdims=True), jnp.max(extra, axis=1, keepdims=True)
            )
            top = top * scale
            cached = jnp.exp2(cached * scale - top)
            extra = jnp.exp2(extra * scale - top)
            total = jnp.sum(cached, axis=1, keepdims=True) + jnp.sum(extra, axis=1, keepdims=True)
            inverse = 1.0 / total
            weights = jnp.concatenate([cached * inverse, extra * inverse], axis=1)
            result = jnp.dot(
                weights.astype(jnp.bfloat16),
                v_v[slot, c, :, k * HD : (k + 1) * HD],
                preferred_element_type=jnp.float32,
            )
            return result.astype(jnp.bfloat16)

        results = []
        ahead = score(units[0])
        for n, unit in enumerate(units):
            scores = ahead
            if n + 1 < len(units):
                ahead = score(units[n + 1])
            results.append(attend(unit, scores))
        for unit, result in zip(units, results):
            _, k, at, _, _, _ = unit
            for h in range(group):
                head = (k * group + h) * HD
                pad_v[at, head : head + HD] = result[h * tall : (h + 1) * tall]
        return carry

    lax.fori_loop(0, pairs, pair_body, 0)
    for half in range(2):
        draft_copy(half).start()

    for c in range(head_cols // WIDE):
        lanes = slice(c * WIDE, (c + 1) * WIDE)
        row_v[:, lanes] = jnp.dot(
            gather_v[...], pad_v[:, lanes], preferred_element_type=jnp.float32
        ).astype(jnp.bfloat16)
    pl.semaphore_wait(barrier, dp_count)

    def partial_copy(c):
        slot = lax.rem(c, SENDS)
        return pltpu.make_async_remote_copy(
            src_ref=send_v.at[slot],
            dst_ref=recv_v.at[c],
            send_sem=send_sem.at[slot],
            recv_sem=recv_sem.at[c],
            device_id=(me, other),
            device_id_type=MESH,
        )

    def send_side(c, carry):
        weight_copy(c).wait()
        partial = jnp.dot(row_v[...], weight_v[c], preferred_element_type=jnp.float32)

        @pl.when(c >= SENDS)
        def _():
            partial_copy(c - SENDS).wait_send()

        send_v[lax.rem(c, SENDS)] = partial
        partial_copy(c).start()
        return carry

    lax.fori_loop(0, chunks, send_side, 0)
    square_v[...] = jnp.zeros(square_v.shape, jnp.float32)
    residual_copy.wait()

    def own_side(c, carry):
        weight_copy(c + chunks).wait()
        own = jnp.dot(row_v[...], weight_v[c + chunks], preferred_element_type=jnp.float32)
        at = pl.ds(pl.multiple_of(c * WIDE, WIDE), WIDE)
        own += hidden_v[:, at].astype(jnp.float32)
        partial_copy(c).wait_recv()
        hidden = (own + recv_v[c]).astype(jnp.bfloat16).astype(jnp.float32)
        squares = hidden * hidden
        part = square_v[...]
        for j in range(WIDE // HD):
            part += squares[:, j * HD : (j + 1) * HD]
        square_v[...] = part
        hidden_v[:, at] = (hidden * gain_ref[:, at]).astype(jnp.bfloat16)
        return carry

    lax.fori_loop(0, chunks, own_side, 0)

    def exchange(src, dst, n):
        return pltpu.make_async_remote_copy(
            src_ref=src,
            dst_ref=dst,
            send_sem=ex_send_sem.at[n],
            recv_sem=ex_recv_sem.at[n],
            device_id=(me, other),
            device_id_type=MESH,
        )

    square_copy = exchange(square_v, square_recv, 0)
    square_copy.start()
    draft_copy(0).wait()
    ex_send[...] = jnp.dot(hidden_v[...], draft_v[0], preferred_element_type=jnp.float32)
    draft_out = exchange(ex_send, ex_recv, 1)
    draft_out.start()
    draft_copy(1).wait()
    projected = jnp.dot(hidden_v[...], draft_v[1], preferred_element_type=jnp.float32)
    kept = jnp.dot(gather_v[...], keep_v[...], preferred_element_type=jnp.float32)
    square_copy.wait_recv()
    total = jnp.sum(square_v[...] + square_recv[...], axis=1, keepdims=True)
    factor = lax.rsqrt(total * (1.0 / width) + 1e-05)
    draft_out.wait_recv()
    projected = (projected + ex_recv[...]) * factor
    new_rows = jnp.where(kept[:, :1] > 0.5, projected, 0.0).astype(jnp.bfloat16)
    packets = jnp.dot(perm_v[...], new_rows, preferred_element_type=jnp.float32)
    packets = packets.astype(jnp.bfloat16)
    for j in range(quarters):
        piece = packets[:, j * HD : (j + 1) * HD]
        packet_v[:, :, j] = piece.reshape(dp_count, steps, peer_rows, HD)

    def row_copy(src, dst, peer):
        return pltpu.make_async_remote_copy(
            src_ref=src,
            dst_ref=dst,
            send_sem=row_send_sem,
            recv_sem=row_recv_sem,
            device_id=(peer, core),
            device_id_type=MESH,
        )

    side = round(dp_count ** (1 / 3))
    digits = [[lax.rem(me // side**a + d, side) * side**a for d in range(side)] for a in range(3)]
    hops = [min(d, side - d) for d in range(side)]
    offsets = [(a, b, c) for a in range(side) for b in range(side) for c in range(side)]
    offsets.sort(key=lambda o: -sum(hops[d] for d in o))
    top, low = me // fold, lax.rem(me, fold)
    for a, b, c in offsets[:-1]:
        peer = digits[2][a] + digits[1][b] + digits[0][c]
        row_copy(packet_v.at[peer], out_ref.at[:, top, :, low], peer).start()
    out_ref[:, top, :, low] = packet_v[me]

    for c in range(max(0, chunks - SENDS), chunks):
        partial_copy(c).wait_send()
    square_copy.wait_send()
    draft_out.wait_send()
    most = pl.ds(0, dp_count - 1)
    everything = row_copy(packet_v.at[most], packet_v.at[most], other)
    everything.wait_send()
    everything.wait_recv()


def body(
    queries, new_kv, kv_cache, context_len, accepted, residual, out_weight, draft_gain, draft_weight
):
    dp_count = lax.axis_size("dp")
    steps, conv, block, head_cols = queries.shape
    ctx, kv_cols = kv_cache.shape[2:]
    d_cols = residual.shape[3]
    width = out_weight.shape[1]
    own_cols = draft_weight.shape[1] // 2
    quarters = own_cols // HD
    rows = steps * conv * block
    padded = steps * conv * PADDED
    peer_rows = -(-(conv * block) // dp_count)
    fold = 8 // peer_rows
    chunks = d_cols // WIDE
    anywhere = pl.BlockSpec(memory_space=pl.ANY)
    smem = pl.BlockSpec(memory_space=pltpu.SMEM)
    vmem = pl.BlockSpec(memory_space=pltpu.VMEM)
    bf16, f32 = jnp.bfloat16, jnp.float32
    received = pl.pallas_call(
        functools.partial(fused_kernel, width=width, steps=steps, conv=conv, block=block),
        out_shape=jax.ShapeDtypeStruct(
            (steps, dp_count // fold, quarters, fold, peer_rows, HD), bf16
        ),
        in_specs=[smem, smem, vmem] + [anywhere] * 6,
        out_specs=vmem,
        scratch_shapes=[
            pltpu.VMEM((rows, head_cols), bf16),
            pltpu.VMEM((padded, head_cols), bf16),
            pltpu.VMEM((steps, 2, conv * block, kv_cols), bf16),
            pltpu.VMEM((2, padded, kv_cols), bf16),
            pltpu.VMEM((SLOTS, 2, ctx + EXTRA, kv_cols), bf16),
            pltpu.VMEM((SLOTS, 2, ctx + EXTRA, kv_cols), bf16),
            pltpu.VMEM((rows, d_cols), bf16),
            pltpu.VMEM((2 * chunks, head_cols, WIDE), bf16),
            pltpu.VMEM((2, d_cols, own_cols), bf16),
            pltpu.VMEM((padded, rows), bf16),
            pltpu.VMEM((rows, padded), bf16),
            pltpu.VMEM((dp_count * steps * peer_rows, rows), bf16),
            pltpu.VMEM((padded, HD), bf16),
            pltpu.VMEM((SENDS, rows, WIDE), f32),
            pltpu.VMEM((chunks, rows, WIDE), f32),
            pltpu.VMEM((rows, HD), f32),
            pltpu.VMEM((rows, HD), f32),
            pltpu.VMEM((rows, own_cols), f32),
            pltpu.VMEM((rows, own_cols), f32),
            pltpu.VMEM((dp_count, steps, quarters, peer_rows, HD), bf16),
            pltpu.SemaphoreType.DMA((3,)),
            pltpu.SemaphoreType.DMA((2, SLOTS)),
            pltpu.SemaphoreType.DMA((2 * chunks,)),
            pltpu.SemaphoreType.DMA((2,)),
            pltpu.SemaphoreType.DMA((SENDS,)),
            pltpu.SemaphoreType.DMA((chunks,)),
            pltpu.SemaphoreType.DMA((2,)),
            pltpu.SemaphoreType.DMA((2,)),
            pltpu.SemaphoreType.DMA,
            pltpu.SemaphoreType.DMA,
        ],
        compiler_params=pltpu.CompilerParams(
            collective_id=0, has_side_effects=True, vmem_limit_bytes=67043328
        ),
        name="verify_and_draft",
    )(
        context_len,
        accepted,
        draft_gain.reshape(1, d_cols),
        queries.transpose(0, 2, 1, 3).reshape(rows, head_cols),
        new_kv.transpose(0, 1, 3, 2, 4).reshape(steps, 2, conv * block, kv_cols),
        kv_cache,
        residual.transpose(0, 2, 1, 3).reshape(rows, d_cols),
        out_weight,
        draft_weight,
    )
    by_row = received.transpose(0, 1, 3, 4, 2, 5)
    return by_row.reshape(steps, dp_count * peer_rows, own_cols)


def solution(mesh):
    in_specs = (
        P(None, "dp", None, "tensor"),
        P(None, None, "dp", None, "tensor"),
        P(None, "dp", None, "tensor"),
        P("dp"),
        P(),
        P(None, "dp", None, "tensor"),
        P("tensor", None),
        P("tensor"),
        P("tensor", None),
    )
    out_specs = P(None, "dp", "tensor")
    return jax.shard_map(body, mesh=mesh, in_specs=in_specs, out_specs=out_specs, check_vma=False)
```

```python
import functools

import jax
import jax.numpy as jnp
from jax import lax
from jax.experimental import pallas as pl
from jax.experimental.pallas import tpu as pltpu
from jax.sharding import PartitionSpec as P

HD = 128
PADDED = 8
EXTRA = 128
SLOTS = 3
GROUP = 2
SENDS = 4
AHEAD = 2
WIDE = 512
MESH = pl.DeviceIdType.MESH


def split_index(x, n):
    if n & (n - 1) == 0:
        shift = n.bit_length() - 1
        return x >> shift, x & (n - 1)
    if n == 7:
        top = (x * 9363) >> 16
        return top, x - top * n
    return x // n, x % n


def one_hot(have, want):
    return jnp.where(have == want, 1.0, 0.0).astype(jnp.bfloat16)


def fused_kernel(
    length_ref,
    accepted_ref,
    gain_ref,
    queries_hbm,
    new_kv_hbm,
    cache_hbm,
    residual_hbm,
    weight_hbm,
    draft_hbm,
    out_ref,
    row_v,
    pad_v,
    new_v,
    extra_v,
    k_v,
    v_v,
    hidden_v,
    weight_v,
    draft_v,
    spread_v,
    gather_v,
    perm_v,
    keep_v,
    send_v,
    recv_v,
    square_v,
    square_recv,
    ex_send,
    ex_recv,
    packet_v,
    first_sem,
    pair_sem,
    weight_sem,
    draft_sem,
    send_sem,
    recv_sem,
    ex_send_sem,
    ex_recv_sem,
    row_send_sem,
    row_recv_sem,
    *,
    width,
    steps,
    conv,
    block,
):
    dp_count = packet_v.shape[0]
    ctx = cache_hbm.shape[2]
    head_cols = queries_hbm.shape[1]
    kv_local = cache_hbm.shape[3] // HD
    group = head_cols // HD // kv_local
    pairs = conv // GROUP
    chunks = recv_v.shape[0]
    step_rows = conv * block
    rows = steps * step_rows
    tall = steps * PADDED
    own_cols = draft_v.shape[2]
    quarters = own_cols // HD
    peer_rows = packet_v.shape[3]
    fold = out_ref.shape[3]
    me = lax.axis_index("dp")
    core = lax.axis_index("tensor")
    other = 1 - core

    def pair_copies(p):
        slot = lax.rem(p, SLOTS)
        span = pl.ds(p * GROUP, GROUP)
        return (
            pltpu.make_async_copy(
                cache_hbm.at[0, span], k_v.at[slot, :, pl.ds(0, ctx)], pair_sem.at[0, slot]
            ),
            pltpu.make_async_copy(
                cache_hbm.at[1, span], v_v.at[slot, :, pl.ds(0, ctx)], pair_sem.at[1, slot]
            ),
        )

    def weight_copy(c):
        side = jnp.where(c < chunks, other, core)
        at = pl.multiple_of(side * (chunks * WIDE) + lax.rem(c, chunks) * WIDE, WIDE)
        return pltpu.make_async_copy(
            weight_hbm.at[:, pl.ds(at, WIDE)], weight_v.at[c], weight_sem.at[c]
        )

    def draft_copy(half):
        side = other if half == 0 else core
        at = pl.multiple_of(side * own_cols, own_cols)
        return pltpu.make_async_copy(
            draft_hbm.at[:, pl.ds(at, own_cols)], draft_v.at[half], draft_sem.at[half]
        )

    query_copy = pltpu.make_async_copy(queries_hbm, row_v, first_sem.at[0])
    new_copy = pltpu.make_async_copy(new_kv_hbm, new_v, first_sem.at[1])
    residual_copy = pltpu.make_async_copy(residual_hbm, hidden_v, first_sem.at[2])
    query_copy.start()
    new_copy.start()
    for p in range(min(SLOTS - 1, pairs)):
        for copy in pair_copies(p):
            copy.start()

    barrier = pltpu.get_barrier_semaphore()
    pl.semaphore_signal(barrier, inc=1, device_id=(me, other), device_id_type=MESH)

    def greet(k, carry):
        pl.semaphore_signal(
            barrier, inc=1, device_id=(lax.rem(me + k, dp_count), core), device_id_type=MESH
        )
        return carry

    lax.fori_loop(1, dp_count, greet, 0)

    k_v[:, :, ctx + tall :, :] = jnp.zeros((SLOTS, GROUP, EXTRA - tall, kv_local * HD), jnp.bfloat16)
    v_v[:, :, ctx + tall :, :] = jnp.zeros((SLOTS, GROUP, EXTRA - tall, kv_local * HD), jnp.bfloat16)

    line = lax.broadcasted_iota(jnp.int32, (conv * tall, 1), 0)
    rest, place = split_index(line, PADDED)
    which, step = split_index(rest, steps)
    want = jnp.where(place < block, step * step_rows + place * conv + which, -1)
    spread_v[...] = one_hot(lax.broadcasted_iota(jnp.int32, spread_v.shape, 1), want)
    line = lax.broadcasted_iota(jnp.int32, (1, conv * tall), 1)
    rest, place = split_index(line, PADDED)
    which, step = split_index(rest, steps)
    want = jnp.where(place < block, step * step_rows + place * conv + which, -1)
    gather_v[...] = one_hot(lax.broadcasted_iota(jnp.int32, gather_v.shape, 0), want)

    line = lax.broadcasted_iota(jnp.int32, (perm_v.shape[0], 1), 0)
    rest, slot = split_index(line, peer_rows)
    peer, step = split_index(rest, steps)
    number = slot * dp_count + peer
    which, place = split_index(number, block)
    want = jnp.where(number < step_rows, step * step_rows + place * conv + which, -1)
    perm_v[...] = one_hot(lax.broadcasted_iota(jnp.int32, perm_v.shape, 1), want)

    new_copy.wait()
    for part in range(2):
        extra_v[part] = jnp.dot(
            spread_v[...],
            jnp.concatenate([new_v[s, part] for s in range(steps)], axis=0),
            preferred_element_type=jnp.float32,
        ).astype(jnp.bfloat16)
    query_copy.wait()
    for c in range(head_cols // WIDE):
        lanes = slice(c * WIDE, (c + 1) * WIDE)
        pad_v[:, lanes] = jnp.dot(
            spread_v[...], row_v[:, lanes], preferred_element_type=jnp.float32
        ).astype(jnp.bfloat16)
    residual_copy.start()

    q_rows = group * tall
    scale = HD ** (-0.5) * 1.4426950408889634
    extra_row = lax.broadcasted_iota(jnp.int32, (q_rows, EXTRA), 0)
    extra_col = lax.broadcasted_iota(jnp.int32, (q_rows, EXTRA), 1)
    extra_line = extra_row & (PADDED - 1)
    second = (extra_row & PADDED) != 0
    first_keys = extra_col < PADDED
    own_limit = jnp.where(second == first_keys, -1, extra_line)
    own_limit = jnp.where(extra_col < tall, own_limit, -1)
    from_first = jnp.logical_and(second, first_keys)
    key_line = extra_col & (PADDED - 1)
    cache_col = lax.broadcasted_iota(jnp.int32, (1, ctx), 1)
    tall_line = lax.broadcasted_iota(jnp.int32, (tall, HD), 0)
    weights_each = (2 * chunks) // pairs

    def pair_body(p, carry):
        slot = lax.rem(p, SLOTS)

        @pl.when(p + SLOTS - 1 < pairs)
        def _():
            for copy in pair_copies(p + SLOTS - 1):
                copy.start()

        @pl.when(p >= 1)
        def _():
            for w in range(weights_each):
                weight_copy((p - 1) * weights_each + w).start()

        for copy in pair_copies(p):
            copy.wait()

        units = []
        for c in range(GROUP):
            b = p * GROUP + c
            at = pl.ds(pl.multiple_of(b * tall, tall), tall)
            k_v[slot, c, ctx : ctx + tall, :] = extra_v[0, at, :]
            v_v[slot, c, ctx : ctx + tall, :] = extra_v[1, at, :]
            took = [accepted_ref[s, me * conv + b] for s in range(steps)]
            keep_v[at, :] = jnp.where(
                (tall_line & (PADDED - 1)) <= jnp.where(tall_line < PADDED, took[0], took[1]),
                1.0,
                0.0,
            ).astype(jnp.bfloat16)
            limit = jnp.where(from_first, took[0], own_limit)
            q_wide = pad_v[at, :]
            for k in range(kv_local):
                units.append((c, k, at, cache_col < length_ref[b], key_line <= limit, q_wide))

        def score(unit):
            c, k, _, _, _, q_wide = unit
            q = jnp.concatenate(
                [q_wide[:, (k * group + h) * HD : (k * group + h + 1) * HD] for h in range(group)],
                axis=0,
            )
            return lax.dot_general(
                q,
                k_v[slot, c, :, k * HD : (k + 1) * HD],
                (((1,), (1,)), ((), ())),
                preferred_element_type=jnp.float32,
            )

        def attend(unit, scores):
            c, k, _, valid, allowed, _ = unit
            cached = jnp.where(valid, scores[:, :ctx], -jnp.inf)
            extra = jnp.where(allowed, scores[:, ctx:], -jnp.inf)
            top = jnp.maximum(
                jnp.max(cached, axis=1, keepdims=True), jnp.max(extra, axis=1, keepdims=True)
            )
            top = top * scale
            cached = jnp.exp2(cached * scale - top)
            extra = jnp.exp2(extra * scale - top)
            total = jnp.sum(cached, axis=1, keepdims=True) + jnp.sum(extra, axis=1, keepdims=True)
            inverse = 1.0 / total
            weights = jnp.concatenate([cached * inverse, extra * inverse], axis=1)
            result = jnp.dot(
                weights.astype(jnp.bfloat16),
                v_v[slot, c, :, k * HD : (k + 1) * HD],
                preferred_element_type=jnp.float32,
            )
            return result.astype(jnp.bfloat16)

        results = []
        ahead = [score(unit) for unit in units[:AHEAD]]
        for n, unit in enumerate(units):
            if n + AHEAD < len(units):
                ahead.append(score(units[n + AHEAD]))
            results.append(attend(unit, ahead[n]))
        for unit, result in zip(units, results):
            _, k, at, _, _, _ = unit
            for h in range(group):
                head = (k * group + h) * HD
                pad_v[at, head : head + HD] = result[h * tall : (h + 1) * tall]
        return carry

    lax.fori_loop(0, pairs, pair_body, 0)
    for w in range(weights_each):
        weight_copy((pairs - 1) * weights_each + w).start()
    for half in range(2):
        draft_copy(half).start()

    for c in range(head_cols // WIDE):
        lanes = slice(c * WIDE, (c + 1) * WIDE)
        row_v[:, lanes] = jnp.dot(
            gather_v[...], pad_v[:, lanes], preferred_element_type=jnp.float32
        ).astype(jnp.bfloat16)
    pl.semaphore_wait(barrier, dp_count)

    def partial_copy(c):
        slot = lax.rem(c, SENDS)
        return pltpu.make_async_remote_copy(
            src_ref=send_v.at[slot],
            dst_ref=recv_v.at[c],
            send_sem=send_sem.at[slot],
            recv_sem=recv_sem.at[c],
            device_id=(me, other),
            device_id_type=MESH,
        )

    def send_side(c, carry):
        weight_copy(c).wait()
        partial = jnp.dot(row_v[...], weight_v[c], preferred_element_type=jnp.float32)

        @pl.when(c >= SENDS)
        def _():
            partial_copy(c - SENDS).wait_send()

        send_v[lax.rem(c, SENDS)] = partial
        partial_copy(c).start()
        return carry

    lax.fori_loop(0, chunks, send_side, 0)
    square_v[...] = jnp.zeros(square_v.shape, jnp.float32)
    residual_copy.wait()

    def own_side(c, carry):
        weight_copy(c + chunks).wait()
        own = jnp.dot(row_v[...], weight_v[c + chunks], preferred_element_type=jnp.float32)
        at = pl.ds(pl.multiple_of(c * WIDE, WIDE), WIDE)
        own += hidden_v[:, at].astype(jnp.float32)
        partial_copy(c).wait_recv()
        hidden = (own + recv_v[c]).astype(jnp.bfloat16).astype(jnp.float32)
        squares = hidden * hidden
        part = square_v[...]
        for j in range(WIDE // HD):
            part += squares[:, j * HD : (j + 1) * HD]
        square_v[...] = part
        hidden_v[:, at] = (hidden * gain_ref[:, at]).astype(jnp.bfloat16)
        return carry

    lax.fori_loop(0, chunks, own_side, 0)

    def exchange(src, dst, n):
        return pltpu.make_async_remote_copy(
            src_ref=src,
            dst_ref=dst,
            send_sem=ex_send_sem.at[n],
            recv_sem=ex_recv_sem.at[n],
            device_id=(me, other),
            device_id_type=MESH,
        )

    square_copy = exchange(square_v, square_recv, 0)
    square_copy.start()
    draft_copy(0).wait()
    ex_send[...] = jnp.dot(hidden_v[...], draft_v[0], preferred_element_type=jnp.float32)
    draft_out = exchange(ex_send, ex_recv, 1)
    draft_out.start()
    draft_copy(1).wait()
    projected = jnp.dot(hidden_v[...], draft_v[1], preferred_element_type=jnp.float32)
    kept = jnp.dot(gather_v[...], keep_v[...], preferred_element_type=jnp.float32)
    square_copy.wait_recv()
    total = jnp.sum(square_v[...] + square_recv[...], axis=1, keepdims=True)
    factor = lax.rsqrt(total * (1.0 / width) + 1e-05)
    draft_out.wait_recv()
    projected = (projected + ex_recv[...]) * factor
    new_rows = jnp.where(kept[:, :1] > 0.5, projected, 0.0).astype(jnp.bfloat16)
    packets = jnp.dot(perm_v[...], new_rows, preferred_element_type=jnp.float32)
    packets = packets.astype(jnp.bfloat16)
    for j in range(quarters):
        piece = packets[:, j * HD : (j + 1) * HD]
        packet_v[:, :, j] = piece.reshape(dp_count, steps, peer_rows, HD)

    def row_copy(src, dst, peer):
        return pltpu.make_async_remote_copy(
            src_ref=src,
            dst_ref=dst,
            send_sem=row_send_sem,
            recv_sem=row_recv_sem,
            device_id=(peer, core),
            device_id_type=MESH,
        )

    side = round(dp_count ** (1 / 3))
    digits = [[lax.rem(me // side**a + d, side) * side**a for d in range(side)] for a in range(3)]
    hops = [min(d, side - d) for d in range(side)]
    offsets = [(a, b, c) for a in range(side) for b in range(side) for c in range(side)]
    offsets.sort(key=lambda o: -sum(hops[d] for d in o))
    top, low = me // fold, lax.rem(me, fold)
    for a, b, c in offsets[:-1]:
        peer = digits[2][a] + digits[1][b] + digits[0][c]
        row_copy(packet_v.at[peer], out_ref.at[:, top, :, low], peer).start()
    out_ref[:, top, :, low] = packet_v[me]

    for c in range(max(0, chunks - SENDS), chunks):
        partial_copy(c).wait_send()
    square_copy.wait_send()
    draft_out.wait_send()
    most = pl.ds(0, dp_count - 1)
    everything = row_copy(packet_v.at[most], packet_v.at[most], other)
    everything.wait_send()
    everything.wait_recv()


def body(
    queries, new_kv, kv_cache, context_len, accepted, residual, out_weight, draft_gain, draft_weight
):
    dp_count = lax.axis_size("dp")
    steps, conv, block, head_cols = queries.shape
    ctx, kv_cols = kv_cache.shape[2:]
    d_cols = residual.shape[3]
    width = out_weight.shape[1]
    own_cols = draft_weight.shape[1] // 2
    quarters = own_cols // HD
    rows = steps * conv * block
    padded = steps * conv * PADDED
    peer_rows = -(-(conv * block) // dp_count)
    fold = 8 // peer_rows
    chunks = d_cols // WIDE
    anywhere = pl.BlockSpec(memory_space=pl.ANY)
    smem = pl.BlockSpec(memory_space=pltpu.SMEM)
    vmem = pl.BlockSpec(memory_space=pltpu.VMEM)
    bf16, f32 = jnp.bfloat16, jnp.float32
    received = pl.pallas_call(
        functools.partial(fused_kernel, width=width, steps=steps, conv=conv, block=block),
        out_shape=jax.ShapeDtypeStruct(
            (steps, dp_count // fold, quarters, fold, peer_rows, HD), bf16
        ),
        in_specs=[smem, smem, vmem] + [anywhere] * 6,
        out_specs=vmem,
        scratch_shapes=[
            pltpu.VMEM((rows, head_cols), bf16),
            pltpu.VMEM((padded, head_cols), bf16),
            pltpu.VMEM((steps, 2, conv * block, kv_cols), bf16),
            pltpu.VMEM((2, padded, kv_cols), bf16),
            pltpu.VMEM((SLOTS, GROUP, ctx + EXTRA, kv_cols), bf16),
            pltpu.VMEM((SLOTS, GROUP, ctx + EXTRA, kv_cols), bf16),
            pltpu.VMEM((rows, d_cols), bf16),
            pltpu.VMEM((2 * chunks, head_cols, WIDE), bf16),
            pltpu.VMEM((2, d_cols, own_cols), bf16),
            pltpu.VMEM((padded, rows), bf16),
            pltpu.VMEM((rows, padded), bf16),
            pltpu.VMEM((dp_count * steps * peer_rows, rows), bf16),
            pltpu.VMEM((padded, HD), bf16),
            pltpu.VMEM((SENDS, rows, WIDE), f32),
            pltpu.VMEM((chunks, rows, WIDE), f32),
            pltpu.VMEM((rows, HD), f32),
            pltpu.VMEM((rows, HD), f32),
            pltpu.VMEM((rows, own_cols), f32),
            pltpu.VMEM((rows, own_cols), f32),
            pltpu.VMEM((dp_count, steps, quarters, peer_rows, HD), bf16),
            pltpu.SemaphoreType.DMA((3,)),
            pltpu.SemaphoreType.DMA((2, SLOTS)),
            pltpu.SemaphoreType.DMA((2 * chunks,)),
            pltpu.SemaphoreType.DMA((2,)),
            pltpu.SemaphoreType.DMA((SENDS,)),
            pltpu.SemaphoreType.DMA((chunks,)),
            pltpu.SemaphoreType.DMA((2,)),
            pltpu.SemaphoreType.DMA((2,)),
            pltpu.SemaphoreType.DMA,
            pltpu.SemaphoreType.DMA,
        ],
        compiler_params=pltpu.CompilerParams(
            collective_id=0, has_side_effects=True, vmem_limit_bytes=67043328
        ),
        name="verify_and_draft",
    )(
        context_len,
        accepted,
        draft_gain.reshape(1, d_cols),
        queries.transpose(0, 2, 1, 3).reshape(rows, head_cols),
        new_kv.transpose(0, 1, 3, 2, 4).reshape(steps, 2, conv * block, kv_cols),
        kv_cache,
        residual.transpose(0, 2, 1, 3).reshape(rows, d_cols),
        out_weight,
        draft_weight,
    )
    by_row = received.transpose(0, 1, 3, 4, 2, 5)
    return by_row.reshape(steps, dp_count * peer_rows, own_cols)


def solution(mesh):
    in_specs = (
        P(None, "dp", None, "tensor"),
        P(None, None, "dp", None, "tensor"),
        P(None, "dp", None, "tensor"),
        P("dp"),
        P(),
        P(None, "dp", None, "tensor"),
        P("tensor", None),
        P("tensor"),
        P("tensor", None),
    )
    out_specs = P(None, "dp", "tensor")
    return jax.shard_map(body, mesh=mesh, in_specs=in_specs, out_specs=out_specs, check_vma=False)
```
